256 devices in a mesh: particle: 4 (over y_hi, core), tile: 64 (over y_lo, z, x).
Axes of the slice: x: 4, y: 4 (y_hi: 2, y_lo: 2; y = y_hi * 2 + y_lo), z: 8, core: 2. Of those that a mesh axis runs over, the one named last changes fastest.
Arguments:
- ensemble: float32 [8, 8, 1024, 2048], P('particle', None, 'tile'), may hold values from -6 to 6
- owners: int32 [8], replicated, may hold values from 0 to 7, as said below
- velocity_x: float32 [8, 1024, 2048], P(None, 'tile'), may hold values from -0.3 to 0.3
- northward_speed_ratio: float32 [8, 1024, 2048], P(None, 'tile'), may hold values from -0.3 to 0.3
- target: float32 [8, 1024, 2048], P(None, 'tile'), may hold values from -6 to 6
- forcing: bfloat16 [2, 8, 8, 1024, 2048], P(None, 'particle', None, 'tile'), may hold values from -6 to 6
- diffusion: float32 [8], replicated, may hold values from 0.05 to 0.2
- nudging: float32 [8], replicated, may hold values from 0.05 to 0.5
- level_depths: float32 [8], replicated, may hold values from 0.25 to 1
Outputs:
- predicted_ensemble_grids: float32 [8, 8, 2048, 1024], P('particle', None, 'tile')
- northward_flux_scaled: float32 [8, 2048, 1024], P('particle', 'tile')
The draws below stay inside these ranges and needn't reach their ends.
Inputs may be any that keep to these rules, and one draw needn't show every extreme that they name: `owners`: 0 and 7 always occur; other members are copied any number of times.
All inputs are finite; a program needn't handle non-finite values.
Results may differ from the reference program's by a relative error of at most 0.0003.
Values sent between devices are 32-bit elements; how exact they have to be, the bound alone decides.
No kernel may reach another device: no remote copies, remote signals or barrier semaphores. Data moves between devices by JAX's collectives and lax.ppermute only.
A program may use at most 128 MiB of HBM per device.

```python
import math
import jax
import jax.numpy as jnp

LAYER_COUNT = 8
NX = 2048
STEPS = 2
MEMBER_COUNT = 8
NY = 1024


def draw_owners(key, part):
    first_key = jax.random.fold_in(key, 11)
    second_key = jax.random.fold_in(key, 23)
    shuffled = jax.random.permutation(first_key, jnp.arange(MEMBER_COUNT, dtype=jnp.int32))
    chosen_members = jax.random.randint(second_key, (MEMBER_COUNT,), 0, MEMBER_COUNT, dtype=jnp.int32)
    keeper = (shuffled == 0) | (shuffled == MEMBER_COUNT - 1)
    return jnp.where(keeper, shuffled, chosen_members).astype(jnp.int32)


def block_levels(stream_key, extent, pieces, least, largest):
    def one(axis_at, parts):
        heights = jax.random.uniform(jax.random.fold_in(jax.random.fold_in(stream_key, 6), axis_at), (parts,), jnp.float32, least / len(pieces), largest / len(pieces))
        return jnp.repeat(jnp.exp(heights), extent[axis_at] // parts).reshape((-1,) + (1,) * (len(extent) - axis_at - 1))

    level = one(*pieces[0])
    for cut in pieces[1:]:
        level = level * one(*cut)
    return level


def gaussian(rng, shape, deviation, limit, cuts=(), kind=jnp.bfloat16):
    result = jax.random.normal(rng, shape, jnp.float32) * deviation
    if len(cuts) > 0:
        result = block_levels(rng, shape, cuts, -0.22, 0.18) * result
    return jnp.clip(result, min=-limit, max=limit).astype(kind)


def setup_inputs(seed: int = 0) -> dict:
    seeds = jax.random.split(jax.random.key(seed), 10)
    ensemble = gaussian(seeds[0], (MEMBER_COUNT, LAYER_COUNT, NY, NX), 1.0, 6.0, ((0, 4), (2, 64)), jnp.float32)
    owners = draw_owners(jax.random.fold_in(seeds[9], 71), 0)
    velocity_x = jnp.clip(jax.random.uniform(seeds[2], (LAYER_COUNT, NY, NX), jnp.float32, -0.3, 0.3) * block_levels(seeds[2], (LAYER_COUNT, NY, NX), ((1, 64),), -0.4, 0.0), -0.3, 0.3)
    northward_speed_ratio = jnp.clip(jax.random.uniform(seeds[3], (LAYER_COUNT, NY, NX), jnp.float32, -0.3, 0.3) * block_levels(seeds[3], (LAYER_COUNT, NY, NX), ((1, 64),), -0.4, 0.0), -0.3, 0.3)
    target = gaussian(seeds[4], (LAYER_COUNT, NY, NX), 1.0, 6.0, ((1, 64),), jnp.float32)
    forcing = gaussian(seeds[5], (STEPS, MEMBER_COUNT, LAYER_COUNT, NY, NX), 1.0, 6.0, ((1, 4), (3, 64)))
    diffusion = jnp.clip(jnp.exp(jax.random.uniform(seeds[6], (LAYER_COUNT,), jnp.float32, math.log(0.05), math.log(0.2))), 0.05, 0.2)
    nudging = jnp.clip(jnp.exp(jax.random.uniform(seeds[7], (LAYER_COUNT,), jnp.float32, math.log(0.05), math.log(0.5))), 0.05, 0.5)
    level_depths = jnp.clip(jnp.exp(jax.random.uniform(seeds[8], (LAYER_COUNT,), jnp.float32, math.log(0.25), math.log(1.0))), 0.25, 1.0)
    return dict(ensemble=ensemble, owners=owners, velocity_x=velocity_x, northward_speed_ratio=northward_speed_ratio, target=target, forcing=forcing, diffusion=diffusion, nudging=nudging, level_depths=level_depths)


forcing_scale = 0.5


def advance(padded, velocity_x, northward_speed_ratio, diffusion, nudging, target, forcing_now):
    center = padded[..., 1:-1, :]
    northern = padded[..., 2:, :]
    southern = padded[..., :-2, :]
    eastern = jnp.roll(center, -1, axis=-1)
    west_boundary = jnp.roll(center, 1, axis=-1)
    laplace = eastern + west_boundary + northern + southern - 4.0 * center
    advect = 0.5 * velocity_x * (eastern - west_boundary) + 0.5 * northward_speed_ratio * (northern - southern)
    return (center - advect + diffusion[:, None, None] * laplace
            + nudging[:, None, None] * (target - center)
            + forcing_scale * forcing_now.astype(jnp.float32))


def reference(ensemble, owners, velocity_x, northward_speed_ratio, target, forcing, diffusion, nudging, level_depths):
    prognostic_tracer = jnp.take(ensemble, owners, axis=0)
    for step_index in range(STEPS):
        padded = jnp.pad(prognostic_tracer, ((0, 0), (0, 0), (1, 1), (0, 0)))
        prognostic_tracer = advance(padded, velocity_x, northward_speed_ratio, diffusion, nudging, target, forcing[step_index])
    predicted_ensemble_grids = jnp.transpose(prognostic_tracer, (0, 1, 3, 2))
    vertical_profile = jnp.sum(level_depths[None, :, None, None] * predicted_ensemble_grids, axis=1)
    northward_flux_scaled = jnp.cumsum(vertical_profile, axis=2) * (NY ** -0.5)
    return (predicted_ensemble_grids, northward_flux_scaled)
```

```python
import jax
import jax.numpy as jnp
from jax import lax
from jax.experimental import pallas as pl
from jax.experimental.pallas import tpu as pltpu
from jax.sharding import PartitionSpec as P


forcing_scale = 0.5
F32 = jnp.float32
MIB = 1 << 20


def params(limit):
    return pltpu.CompilerParams(vmem_limit_bytes=limit * MIB)


def cost(flops, nbytes):
    return pl.CostEstimate(flops=flops, bytes_accessed=nbytes, transcendentals=0)


def combine(f, east, west, n, so, coefs):
    cc, ce, cw, cn, cs = coefs
    return cc * f + (ce * east + cw * west) + (cn * n + cs * so)


def coefs_of(d, nu, u, v):
    hu = 0.5 * u
    hv = 0.5 * v
    return 1.0 - 4.0 * d - nu, d - hu, d + hu, d - hv, d + hv


def sweep(load, edges, coefs, emit, count, lanes, rows):
    row_id = lax.broadcasted_iota(jnp.int32, (rows, 128), 0)
    lane = lax.broadcasted_iota(jnp.int32, (rows, 128), 1)
    turned = []
    for m in range(count):
        last, first = load(m, lanes - 1), load(m, 0)
        turned.append((first, pltpu.roll(last, 1, 1), pltpu.roll(first, 127, 1), pltpu.roll(first, 1, 1)))
    for j in range(lanes):
        now = coefs(j)
        for m in range(count):
            f, prev_right, here_left, here_right = turned[m]
            following = load(m, (j + 1) % lanes)
            next_left = pltpu.roll(following, 127, 1)
            next_right = pltpu.roll(following, 1, 1)
            east = jnp.where(lane == 127, next_left, here_left)
            west = jnp.where(lane == 0, prev_right, here_right)
            turned[m] = (following, here_right, next_left, next_right)
            low, high = edges(m, j)
            up = jnp.where(row_id == rows - 1, high, pltpu.roll(f, rows - 1, 0))
            down = jnp.where(row_id == 0, low, pltpu.roll(f, 1, 0))
            emit(m, j, combine(f, east, west, up, down, now))


def at(j):
    return slice(128 * j, 128 * j + 128)


def table(shape):
    return pl.BlockSpec(shape, lambda *args: (0,) * len(shape))


def pack_static(scal, vx, vy, target, forcing):
    levels, rows, nx = target.shape

    def body(s, u_ref, v_ref, t_ref, w_ref, up_ref, down_ref):
        for ref, r in ((up_ref, rows - 1), (down_ref, 0)):
            for l in range(levels):
                ref[l : l + 1] = u_ref[l, r : r + 1]
                ref[levels + l : levels + l + 1] = v_ref[l, r : r + 1]
                nt = s[8 + l] * t_ref[l, r : r + 1]
                for m in range(2):
                    w = w_ref[0, m, l].astype(F32)[r : r + 1]
                    i = (2 + m) * levels + l
                    ref[i : i + 1] = nt + forcing_scale * w

    shape = (4 * levels, nx)
    out = jax.ShapeDtypeStruct(shape, F32)
    return pl.pallas_call(
        body,
        name="pack_static",
        out_shape=(out, out),
        grid_spec=pltpu.PrefetchScalarGridSpec(
            num_scalar_prefetch=1,
            grid=(1,),
            in_specs=[table(vx.shape)] * 3 + [table((1,) + forcing.shape[1:])],
            out_specs=[table(shape)] * 2,
        ),
        compiler_params=params(60),
        cost_estimate=cost(0, 16 * target.size),
    )(scal, vx, vy, target, forcing)


def pack_edges(ids, parts, limit):
    rows, nx = parts[0].shape[2:]
    total = 8 * len(parts)

    def body(s, *refs):
        up_ref, down_ref = refs[-2:]
        for p, f_ref in enumerate(refs[:-2]):
            for m in range(2):
                for l in range(2):
                    i = ((2 * p + m) * 2 + l) * 2
                    up_ref[i : i + 2] = f_ref[m, l, rows - 2 : rows]
                    down_ref[i : i + 2] = f_ref[m, l, 0:2]

    block = (2, 2, rows, nx)
    in_specs = []
    for part in parts:
        if part.shape[1] == 2:
            in_specs.append(table(block))
        else:
            in_specs.append(pl.BlockSpec(block, lambda i, s: (0, s[8], 0, 0)))
    out = jax.ShapeDtypeStruct((total, nx), F32)
    return pl.pallas_call(
        body,
        name="pack_edges",
        out_shape=(out, out),
        grid_spec=pltpu.PrefetchScalarGridSpec(
            num_scalar_prefetch=1,
            grid=(1,),
            in_specs=in_specs,
            out_specs=[table((total, nx))] * 2,
        ),
        compiler_params=params(limit),
        cost_estimate=cost(0, len(parts) * 16 * rows * nx),
    )(ids, *parts)


def twice(ids, scal, parts, vx, vy, halo, static, before):
    level_count, rows, nx = vx.shape
    lanes = nx // 128
    base = 0 if before is None else 2

    def body(q, s, f0_ref, f1_ref, u_ref, v_ref, below_ref, above_ref, sb_ref, sa_ref, *rest):
        out_ref, cur_ref, mid_ref, low_ref, high_ref = rest[-5:]
        l, p = pl.program_id(0), pl.program_id(1)
        level = 2 * q[8] + l
        d, nu = s[level], s[8 + level]
        low_ok = s[16] > 0.0
        high_ok = s[17] > 0.0

        @pl.when(p == 0)
        def _():
            cur_ref[...] = f0_ref[:, 0]

        @pl.when(p == 1)
        def _():
            cur_ref[...] = f1_ref[:, 0]

        def edge_row(ref, f, n, so):
            u = ref[pl.ds(level, 1), :]
            v = ref[pl.ds(level_count + level, 1), :]
            east = pltpu.roll(f, nx - 1, 1)
            west = pltpu.roll(f, 1, 1)
            return combine(f, east, west, n, so, coefs_of(d, nu, u, v))

        for m in range(2):
            here = ((2 * p + m) * 2 + l) * 2
            s2 = below_ref[pl.ds(here, 1), :]
            s1 = below_ref[pl.ds(here + 1, 1), :]
            n1 = above_ref[pl.ds(here, 1), :]
            n2 = above_ref[pl.ds(here + 1, 1), :]
            new_low = edge_row(sb_ref, s1, cur_ref[m, 0:1, :], s2)
            new_high = edge_row(sa_ref, n1, n2, cur_ref[m, rows - 1 : rows, :])
            low_ref[0, m] = s1
            high_ref[0, m] = n1
            low_ref[1, m] = jnp.where(low_ok, new_low, 0.0)
            high_ref[1, m] = jnp.where(high_ok, new_high, 0.0)

        def coefs(j):
            return coefs_of(d, nu, u_ref[0, :, at(j)], v_ref[0, :, at(j)])

        for step in range(2):

            def load(m, j):
                return mid_ref[m, :, at(j)] if step else cur_ref[m, :, at(j)]

            def edges(m, j):
                return low_ref[step, m, :, at(j)], high_ref[step, m, :, at(j)]

            def emit(m, j, value):
                if step:
                    out_ref[m, 0, :, at(j)] = value
                else:
                    mid_ref[m, :, at(j)] = value

            sweep(load, edges, coefs, emit, 2, lanes, rows)

    one = pl.BlockSpec((1, rows, nx), lambda l, p, q, s: (2 * q[8] + l, 0, 0))
    part_specs = []
    for part in parts:
        if part.shape[1] == 2:
            part_specs.append(pl.BlockSpec((2, 1, rows, nx), lambda l, p, q, s: (0, l, 0, 0)))
        else:
            part_specs.append(
                pl.BlockSpec((2, 1, rows, nx), lambda l, p, q, s: (0, 2 * q[8] + l, 0, 0))
            )
    in_specs = part_specs + [one, one] + [table(h.shape) for h in (*halo, *static)]
    args = [ids, scal, *parts, vx, vy, *halo, *static]
    aliases = {}
    if before is not None:
        aliases = {len(args): 0}
        in_specs.append(pl.BlockSpec(memory_space=pl.ANY))
        args.append(before)
    return pl.pallas_call(
        body,
        name="twice",
        out_shape=jax.ShapeDtypeStruct((8, 2, rows, nx), F32),
        grid_spec=pltpu.PrefetchScalarGridSpec(
            num_scalar_prefetch=2,
            grid=(2, 2),
            in_specs=in_specs,
            out_specs=pl.BlockSpec((2, 1, rows, nx), lambda l, p, q, s: (base + p, l, 0, 0)),
            scratch_shapes=[
                pltpu.VMEM((2, rows, nx), F32),
                pltpu.VMEM((2, rows, nx), F32),
                pltpu.VMEM((2, 2, 1, nx), F32),
                pltpu.VMEM((2, 2, 1, nx), F32),
            ],
        ),
        input_output_aliases=aliases,
        compiler_params=params(16),
        cost_estimate=cost(60 * 8 * rows * nx, 96 * rows * nx),
    )(*args)


def driven(ids, scal, vx, vy, target, forcing, below, above):
    level_count, rows, nx = target.shape
    lanes = nx // 128

    def body(q, s, u_ref, v_ref, t_ref, w_ref, below_ref, above_ref, *rest):
        outs, (src_ref, res_ref, low_ref, high_ref) = rest[:4], rest[4:]
        k, l = 3 - pl.program_id(0), pl.program_id(1)
        level = 2 * q[8 + k] + l
        d, nu = s[level], s[8 + level]
        for m in range(2):
            low_ref[m] = below_ref[pl.ds((2 + m) * level_count + level, 1), :]
            high_ref[m] = above_ref[pl.ds((2 + m) * level_count + level, 1), :]
        for j in range(lanes):
            nt = nu * t_ref[0, :, at(j)]
            for m in range(2):
                src_ref[m, :, at(j)] = nt + forcing_scale * w_ref[0, m, 0, :, at(j)].astype(F32)

        def coefs(j):
            return coefs_of(d, nu, u_ref[0, :, at(j)], v_ref[0, :, at(j)])

        def load(m, j):
            return src_ref[m, :, at(j)]

        def edges(m, j):
            return low_ref[m, :, at(j)], high_ref[m, :, at(j)]

        def emit(m, j, value):
            later = nu * t_ref[0, :, at(j)] + forcing_scale * w_ref[1, m, 0, :, at(j)].astype(F32)
            res_ref[m, :, at(j)] = value + later

        sweep(load, edges, coefs, emit, 2, lanes, rows)
        for value in range(4):

            @pl.when(k == value)
            def _(ref=outs[value]):
                ref[:, 0] = res_ref[...]

    def turn(value):
        def index(k, l, q, s):
            k = 3 - k
            return (0, jnp.where(k == value, l, jnp.where(k > value, 0, 1)), 0, 0)

        return index

    group = lambda k, l, q: 2 * q[8 + 3 - k] + l
    one = pl.BlockSpec((1, rows, nx), lambda k, l, q, s: (group(k, l, q), 0, 0))
    return pl.pallas_call(
        body,
        name="driven",
        out_shape=[jax.ShapeDtypeStruct((2, 2, rows, nx), F32)] * 4,
        grid_spec=pltpu.PrefetchScalarGridSpec(
            num_scalar_prefetch=2,
            grid=(4, 2),
            in_specs=[
                one,
                one,
                one,
                pl.BlockSpec(
                    (2, 2, 1, rows, nx), lambda k, l, q, s: (0, 0, group(k, l, q), 0, 0)
                ),
                table(below.shape),
                table(above.shape),
            ],
            out_specs=[pl.BlockSpec((2, 1, rows, nx), turn(value)) for value in range(4)],
            scratch_shapes=[
                pltpu.VMEM((2, rows, nx), F32),
                pltpu.VMEM((2, rows, nx), F32),
                pltpu.VMEM((2, 1, nx), F32),
                pltpu.VMEM((2, 1, nx), F32),
            ],
        ),
        compiler_params=params(16),
        cost_estimate=cost(40 * 2 * target.size, 28 * target.size),
    )(ids, scal, vx, vy, target, forcing, below, above)


def assemble(ids, moved, rests, tiles):
    _, _, rows, nx = moved.shape
    cols = nx // tiles
    per = 128 // cols

    def body(s, f0_ref, f1_ref, r0_ref, r1_ref, r2_ref, r3_ref, out_ref, sum_ref):
        k = pl.program_id(0)
        lane = lax.broadcasted_iota(jnp.int32, (rows, 128), 1)
        for value, ref in enumerate((r0_ref, r1_ref, r2_ref, r3_ref)):

            @pl.when(k == value)
            def _(ref=ref):
                sum_ref[0] = f0_ref[0] + ref[0]
                sum_ref[1] = f1_ref[0] + ref[1]

        for j in range(nx // 128):
            pieces = [sum_ref[m, l, :, at(j)] for m in range(2) for l in range(2)]
            for q in range(per):
                block = None
                for i in range(4):
                    shift = ((i - q) * cols) % 128
                    moved = pltpu.roll(pieces[i], shift, 1) if shift else pieces[i]
                    block = moved if block is None else jnp.where(lane >= i * cols, moved, block)
                out_ref[0, per * j + q] = block

    one = (1, 2, rows, nx)
    return pl.pallas_call(
        body,
        name="assemble",
        out_shape=jax.ShapeDtypeStruct((4, tiles, rows, 128), F32),
        grid_spec=pltpu.PrefetchScalarGridSpec(
            num_scalar_prefetch=1,
            grid=(4,),
            in_specs=[
                pl.BlockSpec(one, lambda k, s: (s[2 * k], 0, 0, 0)),
                pl.BlockSpec(one, lambda k, s: (s[2 * k + 1], 0, 0, 0)),
            ]
            + [table((2, 2, rows, nx))] * 4,
            out_specs=pl.BlockSpec((1, tiles, rows, 128), lambda k, s: (s[8 + k], 0, 0, 0)),
            scratch_shapes=[pltpu.VMEM((2, 2, rows, nx), F32)],
        ),
        compiler_params=params(20),
        cost_estimate=cost(moved.size, 16 * moved.size),
    )(ids, moved, moved, *rests)


def finish(depths, arrived, ny):
    pairs, tiles, rows, _ = arrived.shape
    levels = 2 * pairs
    group = 128 // rows
    blocks = 2 if tiles % (2 * group) == 0 else 1
    steps = tiles // (group * blocks)
    width = 128 * blocks
    scale = ny ** (-0.5)

    def body(s, a_ref, out_ref, sum_ref, carry):
        @pl.when(pl.program_id(0) == 0)
        def _():
            carry[...] = jnp.zeros_like(carry)

        r = lax.broadcasted_iota(jnp.int32, (128, 128), 0)
        c = lax.broadcasted_iota(jnp.int32, (128, 128), 1)
        tri = (r <= c).astype(jnp.bfloat16)
        for b in range(blocks):
            lanes = slice(128 * b, 128 * b + 128)
            total = None
            for lp in range(pairs):
                x = a_ref[lp, group * b : group * (b + 1)].reshape(128, 128).T
                x = x.reshape(2, 2, 32, 128)
                for k in range(2):
                    level = 2 * lp + k
                    out_ref[:, level, :, lanes] = x[:, k]
                    term = s[level] * x[:, k]
                    total = term if total is None else total + term
            total = total.reshape(64, 128)
            hi = total.astype(jnp.bfloat16)
            lo = (total - hi.astype(F32)).astype(jnp.bfloat16)
            run = jnp.dot(hi, tri, preferred_element_type=F32) + jnp.dot(
                lo, tri, preferred_element_type=F32
            )
            run = run + carry[...]
            carry[...] = jnp.broadcast_to(run[:, 127:128], (64, 128))
            sum_ref[:, :, lanes] = (run * scale).reshape(2, 32, 128)

    return pl.pallas_call(
        body,
        name="finish",
        out_shape=(
            jax.ShapeDtypeStruct((2, levels, 32, ny), F32),
            jax.ShapeDtypeStruct((2, 32, ny), F32),
        ),
        grid_spec=pltpu.PrefetchScalarGridSpec(
            num_scalar_prefetch=1,
            grid=(steps,),
            in_specs=[pl.BlockSpec((pairs, group * blocks, rows, 128), lambda i, s: (0, i, 0, 0))],
            out_specs=[
                pl.BlockSpec((2, levels, 32, width), lambda i, s: (0, 0, 0, i)),
                pl.BlockSpec((2, 32, width), lambda i, s: (0, 0, i)),
            ],
            scratch_shapes=[pltpu.VMEM((64, 128), F32)],
        ),
        compiler_params=params(16),
        cost_estimate=cost(20 * arrived.size, 12 * arrived.size),
    )(depths, arrived)


def on_device(
    ensemble,
    owners,
    velocity_x,
    northward_speed_ratio,
    target,
    forcing,
    diffusion,
    nudging,
    level_depths,
):
    tiles = lax.axis_size("tile")
    rows, _ = ensemble.shape[2:]
    group = lax.axis_index("particle")
    tile = lax.axis_index("tile")
    up = [(i, i + 1) for i in range(tiles - 1)]
    down = [(i + 1, i) for i in range(tiles - 1)]

    def trade(value, k):
        return lax.ppermute(value, "particle", [(i, i ^ k) for i in range(4)])

    parts = [ensemble, None, None, None]
    for k in (1, 3, 2):
        piece = lax.dynamic_slice_in_dim(ensemble, 2 * (group ^ k), 2, axis=1)
        parts[k] = trade(piece, k)

    others = group ^ jnp.arange(4, dtype=jnp.int32)
    wanted = jnp.take(owners.reshape(4, 2), others, axis=0).reshape(8)
    slots = 2 * ((wanted >> 1) ^ group) + (wanted & 1)
    ids = jnp.concatenate([slots, others]).astype(jnp.int32)
    edges_ok = jnp.stack([tile > 0, tile < tiles - 1]).astype(F32)
    scal = jnp.concatenate([diffusion, nudging, edges_ok])

    def exchange(pair):
        below = lax.ppermute(pair[0], "tile", up)
        above = lax.ppermute(pair[1], "tile", down)
        return below, above

    edges = pack_static(scal, velocity_x, northward_speed_ratio, target, forcing)
    static = exchange(edges)
    edges = pack_edges(ids, parts[:2], 60)
    near = exchange(edges)
    rests = driven(
        ids, scal, velocity_x, northward_speed_ratio, target, forcing, *static
    )
    rests = list(rests)
    for k in (3, 2, 1):
        rests[k] = trade(rests[k], k)
    moved = twice(
        ids, scal, parts[:2], velocity_x, northward_speed_ratio, near, static, None
    )
    edges = pack_edges(ids, parts[2:], 16)
    far = exchange(edges)
    moved = twice(
        ids, scal, parts[2:], velocity_x, northward_speed_ratio, far, static, moved
    )
    blocks = assemble(ids, moved, rests, tiles)
    arrived = lax.all_to_all(
        blocks.reshape(4 * tiles, rows, 128), ("particle", "tile"), 0, 0, tiled=True
    )
    return finish(level_depths, arrived.reshape(4, tiles, rows, 128), tiles * rows)


def solution(mesh):
    placed = (
        P("particle", None, "tile", None),
        P(),
        P(None, "tile", None),
        P(None, "tile", None),
        P(None, "tile", None),
        P(None, "particle", None, "tile", None),
        P(),
        P(),
        P(),
    )
    return jax.shard_map(
        on_device,
        mesh=mesh,
        in_specs=placed,
        out_specs=(P("particle", None, "tile", None), P("particle", "tile", None)),
        check_vma=False,
    )
```

```python
import jax
import jax.numpy as jnp
from jax import lax
from jax.experimental import pallas as pl
from jax.experimental.pallas import tpu as pltpu
from jax.sharding import PartitionSpec as P


forcing_scale = 0.5
F32 = jnp.float32
MIB = 1 << 20


def params(limit):
    return pltpu.CompilerParams(vmem_limit_bytes=limit * MIB)


def cost(flops, nbytes):
    return pl.CostEstimate(flops=flops, bytes_accessed=nbytes, transcendentals=0)


def combine(f, east, west, n, so, coefs):
    cc, ce, cw, cn, cs = coefs
    return cc * f + (ce * east + cw * west) + (cn * n + cs * so)


def coefs_of(d, nu, u, v):
    hu = 0.5 * u
    hv = 0.5 * v
    return 1.0 - 4.0 * d - nu, d - hu, d + hu, d - hv, d + hv


def sweep(load, edges, coefs, emit, count, lanes, rows):
    row_id = lax.broadcasted_iota(jnp.int32, (rows, 128), 0)
    lane = lax.broadcasted_iota(jnp.int32, (rows, 128), 1)
    turned = []
    for m in range(count):
        last, first = load(m, lanes - 1), load(m, 0)
        turned.append((first, pltpu.roll(last, 1, 1), pltpu.roll(first, 127, 1), pltpu.roll(first, 1, 1)))
    for j in range(lanes):
        now = coefs(j)
        for m in range(count):
            f, prev_right, here_left, here_right = turned[m]
            following = load(m, (j + 1) % lanes)
            next_left = pltpu.roll(following, 127, 1)
            next_right = pltpu.roll(following, 1, 1)
            east = jnp.where(lane == 127, next_left, here_left)
            west = jnp.where(lane == 0, prev_right, here_right)
            turned[m] = (following, here_right, next_left, next_right)
            low, high = edges(m, j)
            up = jnp.where(row_id == rows - 1, high, pltpu.roll(f, rows - 1, 0))
            down = jnp.where(row_id == 0, low, pltpu.roll(f, 1, 0))
            emit(m, j, combine(f, east, west, up, down, now))


def at(j):
    return slice(128 * j, 128 * j + 128)


def table(shape):
    return pl.BlockSpec(shape, lambda *args: (0,) * len(shape))


def pack_static(scal, vx, vy, target, forcing):
    levels, rows, nx = target.shape

    def body(s, u_ref, v_ref, t_ref, w_ref, up_ref, down_ref):
        for ref, r in ((up_ref, rows - 1), (down_ref, 0)):
            for l in range(levels):
                ref[l : l + 1] = u_ref[l, r : r + 1]
                ref[levels + l : levels + l + 1] = v_ref[l, r : r + 1]
                nt = s[8 + l] * t_ref[l, r : r + 1]
                for m in range(2):
                    w = w_ref[0, m, l, r : r + 1].astype(F32)
                    i = (2 + m) * levels + l
                    ref[i : i + 1] = nt + forcing_scale * w

    shape = (4 * levels, nx)
    out = jax.ShapeDtypeStruct(shape, F32)
    return pl.pallas_call(
        body,
        name="pack_static",
        out_shape=(out, out),
        grid_spec=pltpu.PrefetchScalarGridSpec(
            num_scalar_prefetch=1,
            grid=(1,),
            in_specs=[table(vx.shape)] * 3 + [table((1,) + forcing.shape[1:])],
            out_specs=[table(shape)] * 2,
        ),
        compiler_params=params(16),
        cost_estimate=cost(0, 16 * target.size),
    )(scal, vx, vy, target, forcing)


def pack_edges(ids, parts, limit):
    rows, nx = parts[0].shape[2:]
    total = 8 * len(parts)

    def body(s, *refs):
        up_ref, down_ref = refs[-2:]
        for p, f_ref in enumerate(refs[:-2]):
            for m in range(2):
                for l in range(2):
                    i = ((2 * p + m) * 2 + l) * 2
                    up_ref[i : i + 2] = f_ref[m, l, rows - 2 : rows]
                    down_ref[i : i + 2] = f_ref[m, l, 0:2]

    block = (2, 2, rows, nx)
    in_specs = []
    for part in parts:
        if part.shape[1] == 2:
            in_specs.append(table(block))
        else:
            in_specs.append(pl.BlockSpec(block, lambda i, s: (0, s[8], 0, 0)))
    out = jax.ShapeDtypeStruct((total, nx), F32)
    return pl.pallas_call(
        body,
        name="pack_edges",
        out_shape=(out, out),
        grid_spec=pltpu.PrefetchScalarGridSpec(
            num_scalar_prefetch=1,
            grid=(1,),
            in_specs=in_specs,
            out_specs=[table((total, nx))] * 2,
        ),
        compiler_params=params(limit),
        cost_estimate=cost(0, len(parts) * 16 * rows * nx),
    )(ids, *parts)


def twice(ids, scal, parts, vx, vy, halo, static, before):
    level_count, rows, nx = vx.shape
    lanes = nx // 128
    base = 0 if before is None else 2

    def body(q, s, f0_ref, f1_ref, u_ref, v_ref, below_ref, above_ref, sb_ref, sa_ref, *rest):
        out_ref, cur_ref, mid_ref, low_ref, high_ref = rest[-5:]
        l, p = pl.program_id(0), pl.program_id(1)
        level = 2 * q[8] + l
        d, nu = s[level], s[8 + level]
        low_ok = s[16] > 0.0
        high_ok = s[17] > 0.0

        @pl.when(p == 0)
        def _():
            cur_ref[...] = f0_ref[:, 0]

        @pl.when(p == 1)
        def _():
            cur_ref[...] = f1_ref[:, 0]

        def edge_row(ref, f, n, so):
            u = ref[pl.ds(level, 1), :]
            v = ref[pl.ds(level_count + level, 1), :]
            east = pltpu.roll(f, nx - 1, 1)
            west = pltpu.roll(f, 1, 1)
            return combine(f, east, west, n, so, coefs_of(d, nu, u, v))

        for m in range(2):
            here = ((2 * p + m) * 2 + l) * 2
            s2 = below_ref[pl.ds(here, 1), :]
            s1 = below_ref[pl.ds(here + 1, 1), :]
            n1 = above_ref[pl.ds(here, 1), :]
            n2 = above_ref[pl.ds(here + 1, 1), :]
            new_low = edge_row(sb_ref, s1, cur_ref[m, 0:1, :], s2)
            new_high = edge_row(sa_ref, n1, n2, cur_ref[m, rows - 1 : rows, :])
            low_ref[0, m] = s1
            high_ref[0, m] = n1
            low_ref[1, m] = jnp.where(low_ok, new_low, 0.0)
            high_ref[1, m] = jnp.where(high_ok, new_high, 0.0)

        def coefs(j):
            return coefs_of(d, nu, u_ref[0, :, at(j)], v_ref[0, :, at(j)])

        for step in range(2):

            def load(m, j):
                return mid_ref[m, :, at(j)] if step else cur_ref[m, :, at(j)]

            def edges(m, j):
                return low_ref[step, m, :, at(j)], high_ref[step, m, :, at(j)]

            def emit(m, j, value):
                if step:
                    out_ref[m, 0, :, at(j)] = value
                else:
                    mid_ref[m, :, at(j)] = value

            sweep(load, edges, coefs, emit, 2, lanes, rows)

    one = pl.BlockSpec((1, rows, nx), lambda l, p, q, s: (2 * q[8] + l, 0, 0))
    part_specs = []
    for part in parts:
        if part.shape[1] == 2:
            part_specs.append(pl.BlockSpec((2, 1, rows, nx), lambda l, p, q, s: (0, l, 0, 0)))
        else:
            part_specs.append(
                pl.BlockSpec((2, 1, rows, nx), lambda l, p, q, s: (0, 2 * q[8] + l, 0, 0))
            )
    in_specs = part_specs + [one, one] + [table(h.shape) for h in (*halo, *static)]
    args = [ids, scal, *parts, vx, vy, *halo, *static]
    aliases = {}
    if before is not None:
        aliases = {len(args): 0}
        in_specs.append(pl.BlockSpec(memory_space=pl.ANY))
        args.append(before)
    return pl.pallas_call(
        body,
        name="twice",
        out_shape=jax.ShapeDtypeStruct((8, 2, rows, nx), F32),
        grid_spec=pltpu.PrefetchScalarGridSpec(
            num_scalar_prefetch=2,
            grid=(2, 2),
            in_specs=in_specs,
            out_specs=pl.BlockSpec((2, 1, rows, nx), lambda l, p, q, s: (base + p, l, 0, 0)),
            scratch_shapes=[
                pltpu.VMEM((2, rows, nx), F32),
                pltpu.VMEM((2, rows, nx), F32),
                pltpu.VMEM((2, 2, 1, nx), F32),
                pltpu.VMEM((2, 2, 1, nx), F32),
            ],
        ),
        input_output_aliases=aliases,
        compiler_params=params(16),
        cost_estimate=cost(60 * 8 * rows * nx, 96 * rows * nx),
    )(*args)


def driven(ids, scal, vx, vy, target, forcing, below, above):
    level_count, rows, nx = target.shape
    lanes = nx // 128

    def body(q, s, u_ref, v_ref, t_ref, w_ref, below_ref, above_ref, *rest):
        outs, (src_ref, res_ref, low_ref, high_ref) = rest[:4], rest[4:]
        k, l = 3 - pl.program_id(0), pl.program_id(1)
        level = 2 * (q[8] ^ k) + l
        d, nu = s[level], s[8 + level]
        for m in range(2):
            low_ref[m] = below_ref[pl.ds((2 + m) * level_count + level, 1), :]
            high_ref[m] = above_ref[pl.ds((2 + m) * level_count + level, 1), :]
        for j in range(lanes):
            nt = nu * t_ref[0, :, at(j)]
            for m in range(2):
                src_ref[m, :, at(j)] = nt + forcing_scale * w_ref[0, m, 0, :, at(j)].astype(F32)

        def coefs(j):
            return coefs_of(d, nu, u_ref[0, :, at(j)], v_ref[0, :, at(j)])

        def load(m, j):
            return src_ref[m, :, at(j)]

        def edges(m, j):
            return low_ref[m, :, at(j)], high_ref[m, :, at(j)]

        def emit(m, j, value):
            later = nu * t_ref[0, :, at(j)] + forcing_scale * w_ref[1, m, 0, :, at(j)].astype(F32)
            res_ref[m, :, at(j)] = value + later

        sweep(load, edges, coefs, emit, 2, lanes, rows)
        for value in range(4):

            @pl.when(k == value)
            def _(ref=outs[value]):
                ref[:, 0] = res_ref[...]

    def turn(value):
        def index(k, l, q, s):
            k = 3 - k
            return (0, jnp.where(k == value, l, jnp.where(k > value, 0, 1)), 0, 0)

        return index

    group = lambda k, l, q: 2 * (q[8] ^ (3 - k)) + l
    one = pl.BlockSpec((1, rows, nx), lambda k, l, q, s: (group(k, l, q), 0, 0))
    return pl.pallas_call(
        body,
        name="driven",
        out_shape=[jax.ShapeDtypeStruct((2, 2, rows, nx), F32)] * 4,
        grid_spec=pltpu.PrefetchScalarGridSpec(
            num_scalar_prefetch=2,
            grid=(4, 2),
            in_specs=[
                one,
                one,
                one,
                pl.BlockSpec(
                    (2, 2, 1, rows, nx), lambda k, l, q, s: (0, 0, group(k, l, q), 0, 0)
                ),
                table(below.shape),
                table(above.shape),
            ],
            out_specs=[pl.BlockSpec((2, 1, rows, nx), turn(value)) for value in range(4)],
            scratch_shapes=[
                pltpu.VMEM((2, rows, nx), F32),
                pltpu.VMEM((2, rows, nx), F32),
                pltpu.VMEM((2, 1, nx), F32),
                pltpu.VMEM((2, 1, nx), F32),
            ],
        ),
        compiler_params=params(16),
        cost_estimate=cost(40 * 2 * target.size, 28 * target.size),
    )(ids, scal, vx, vy, target, forcing, below, above)


def slot(ids, k, m):
    member = ids[2 * (ids[8] ^ k) + m]
    return 2 * ((member >> 1) ^ ids[8]) + (member & 1)


def assemble(ids, moved, rests, tiles, base, before):
    _, _, rows, nx = moved.shape
    cols = nx // tiles
    per = 128 // cols

    def body(s, f0_ref, f1_ref, r0_ref, r1_ref, *rest):
        out_ref, sum_ref = rest[-2:]
        k = pl.program_id(0)
        lane = lax.broadcasted_iota(jnp.int32, (rows, 128), 1)
        for value, ref in enumerate((r0_ref, r1_ref)):

            @pl.when(k == value)
            def _(ref=ref):
                sum_ref[0] = f0_ref[0] + ref[0]
                sum_ref[1] = f1_ref[0] + ref[1]

        for j in range(nx // 128):
            pieces = [sum_ref[m, l, :, at(j)] for m in range(2) for l in range(2)]
            for q in range(per):
                block = None
                for i in range(4):
                    shift = ((i - q) * cols) % 128
                    moved = pltpu.roll(pieces[i], shift, 1) if shift else pieces[i]
                    block = moved if block is None else jnp.where(lane >= i * cols, moved, block)
                out_ref[0, per * j + q] = block

    one = (1, 2, rows, nx)
    in_specs = [
        pl.BlockSpec(one, lambda k, s: (slot(s, base + k, 0), 0, 0, 0)),
        pl.BlockSpec(one, lambda k, s: (slot(s, base + k, 1), 0, 0, 0)),
    ] + [table((2, 2, rows, nx))] * 2
    args = [ids, moved, moved, *rests]
    aliases = {}
    if before is not None:
        aliases = {len(args): 0}
        in_specs.append(pl.BlockSpec(memory_space=pl.ANY))
        args.append(before)
    return pl.pallas_call(
        body,
        name="assemble",
        out_shape=jax.ShapeDtypeStruct((4, tiles, rows, 128), F32),
        grid_spec=pltpu.PrefetchScalarGridSpec(
            num_scalar_prefetch=1,
            grid=(2,),
            in_specs=in_specs,
            out_specs=pl.BlockSpec((1, tiles, rows, 128), lambda k, s: (s[8] ^ (base + k), 0, 0, 0)),
            scratch_shapes=[pltpu.VMEM((2, 2, rows, nx), F32)],
        ),
        input_output_aliases=aliases,
        compiler_params=params(20),
        cost_estimate=cost(moved.size, 8 * moved.size),
    )(*args)


def finish(depths, arrived, ny):
    pairs, tiles, rows, _ = arrived.shape
    levels = 2 * pairs
    group = 128 // rows
    blocks = 2 if tiles % (2 * group) == 0 else 1
    steps = tiles // (group * blocks)
    width = 128 * blocks
    scale = ny ** (-0.5)

    def body(s, a_ref, out_ref, sum_ref, carry):
        @pl.when(pl.program_id(0) == 0)
        def _():
            carry[...] = jnp.zeros_like(carry)

        r = lax.broadcasted_iota(jnp.int32, (128, 128), 0)
        c = lax.broadcasted_iota(jnp.int32, (128, 128), 1)
        tri = (r <= c).astype(jnp.bfloat16)
        for b in range(blocks):
            lanes = slice(128 * b, 128 * b + 128)
            total = None
            for lp in range(pairs):
                x = a_ref[lp, group * b : group * (b + 1)].reshape(128, 128).T
                x = x.reshape(2, 2, 32, 128)
                for k in range(2):
                    level = 2 * lp + k
                    out_ref[:, level, :, lanes] = x[:, k]
                    term = s[level] * x[:, k]
                    total = term if total is None else total + term
            total = total.reshape(64, 128)
            hi = total.astype(jnp.bfloat16)
            lo = (total - hi.astype(F32)).astype(jnp.bfloat16)
            run = jnp.dot(hi, tri, preferred_element_type=F32) + jnp.dot(
                lo, tri, preferred_element_type=F32
            )
            run = run + carry[...]
            carry[...] = jnp.broadcast_to(run[:, 127:128], (64, 128))
            sum_ref[:, :, lanes] = (run * scale).reshape(2, 32, 128)

    return pl.pallas_call(
        body,
        name="finish",
        out_shape=(
            jax.ShapeDtypeStruct((2, levels, 32, ny), F32),
            jax.ShapeDtypeStruct((2, 32, ny), F32),
        ),
        grid_spec=pltpu.PrefetchScalarGridSpec(
            num_scalar_prefetch=1,
            grid=(steps,),
            in_specs=[pl.BlockSpec((pairs, group * blocks, rows, 128), lambda i, s: (0, i, 0, 0))],
            out_specs=[
                pl.BlockSpec((2, levels, 32, width), lambda i, s: (0, 0, 0, i)),
                pl.BlockSpec((2, 32, width), lambda i, s: (0, 0, i)),
            ],
            scratch_shapes=[pltpu.VMEM((64, 128), F32)],
        ),
        compiler_params=params(16),
        cost_estimate=cost(20 * arrived.size, 12 * arrived.size),
    )(depths, arrived)


def on_device(
    ensemble,
    owners,
    velocity_x,
    northward_speed_ratio,
    target,
    forcing,
    diffusion,
    nudging,
    level_depths,
):
    tiles = lax.axis_size("tile")
    rows, _ = ensemble.shape[2:]
    group = lax.axis_index("particle")
    tile = lax.axis_index("tile")
    up = [(i, i + 1) for i in range(tiles - 1)]
    down = [(i + 1, i) for i in range(tiles - 1)]

    def trade(value, k):
        return lax.ppermute(value, "particle", [(i, i ^ k) for i in range(4)])

    pieces = [lax.dynamic_slice_in_dim(ensemble, 2 * (group ^ k), 2, axis=1) for k in range(4)]
    parts = [pieces[0], None, None, None]
    for k in (3, 2, 1):
        parts[k] = trade(pieces[k], k)

    ids = jnp.concatenate([owners, group[None].astype(jnp.int32)])
    edges_ok = jnp.stack([tile > 0, tile < tiles - 1]).astype(F32)
    scal = jnp.concatenate([diffusion, nudging, edges_ok])

    def exchange(pair):
        below = lax.ppermute(pair[0], "tile", up)
        above = lax.ppermute(pair[1], "tile", down)
        return below, above

    edges = pack_static(scal, velocity_x, northward_speed_ratio, target, forcing)
    static = exchange(edges)
    edges = pack_edges(ids, parts[:2], 16)
    near = exchange(edges)
    rests = driven(
        ids, scal, velocity_x, northward_speed_ratio, target, forcing, *static
    )
    rests = list(rests)
    for k in (3, 2, 1):
        rests[k] = trade(rests[k], k)
    edges = pack_edges(ids, parts[2:], 16)
    far = exchange(edges)
    moved = twice(
        ids, scal, parts[:2], velocity_x, northward_speed_ratio, near, static, None
    )
    moved = twice(
        ids, scal, parts[2:], velocity_x, northward_speed_ratio, far, static, moved
    )
    blocks = assemble(ids, moved, rests[:2], tiles, 0, None)
    blocks = assemble(ids, moved, rests[2:], tiles, 2, blocks)
    arrived = lax.all_to_all(
        blocks.reshape(4 * tiles, rows, 128), ("particle", "tile"), 0, 0, tiled=True
    )
    return finish(level_depths, arrived.reshape(4, tiles, rows, 128), tiles * rows)


def solution(mesh):
    placed = (
        P("particle", None, "tile", None),
        P(),
        P(None, "tile", None),
        P(None, "tile", None),
        P(None, "tile", None),
        P(None, "particle", None, "tile", None),
        P(),
        P(),
        P(),
    )
    return jax.shard_map(
        on_device,
        mesh=mesh,
        in_specs=placed,
        out_specs=(P("particle", None, "tile", None), P("particle", "tile", None)),
        check_vma=False,
    )
```

```python
import jax
import jax.numpy as jnp
from jax import lax
from jax.experimental import pallas as pl
from jax.experimental.pallas import tpu as pltpu
from jax.sharding import PartitionSpec as P


forcing_scale = 0.5
F32 = jnp.float32
MIB = 1 << 20


def params(limit):
    return pltpu.CompilerParams(vmem_limit_bytes=limit * MIB)


def cost(flops, nbytes):
    return pl.CostEstimate(flops=flops, bytes_accessed=nbytes, transcendentals=0)


def combine(f, east, west, n, so, coefs):
    cc, ce, cw, cn, cs = coefs
    return cc * f + (ce * east + cw * west) + (cn * n + cs * so)


def coefs_of(d, nu, u, v):
    hu = 0.5 * u
    hv = 0.5 * v
    return 1.0 - 4.0 * d - nu, d - hu, d + hu, d - hv, d + hv


def sweep(load, edges, coefs, emit, count, lanes, rows):
    row_id = lax.broadcasted_iota(jnp.int32, (rows, 128), 0)
    lane = lax.broadcasted_iota(jnp.int32, (rows, 128), 1)
    turned = []
    for m in range(count):
        last, first = load(m, lanes - 1), load(m, 0)
        turned.append((first, pltpu.roll(last, 1, 1), pltpu.roll(first, 127, 1), pltpu.roll(first, 1, 1)))
    for j in range(lanes):
        now = coefs(j)
        for m in range(count):
            f, prev_right, here_left, here_right = turned[m]
            following = load(m, (j + 1) % lanes)
            next_left = pltpu.roll(following, 127, 1)
            next_right = pltpu.roll(following, 1, 1)
            east = jnp.where(lane == 127, next_left, here_left)
            west = jnp.where(lane == 0, prev_right, here_right)
            turned[m] = (following, here_right, next_left, next_right)
            low, high = edges(m, j)
            up = jnp.where(row_id == rows - 1, high, pltpu.roll(f, rows - 1, 0))
            down = jnp.where(row_id == 0, low, pltpu.roll(f, 1, 0))
            emit(m, j, combine(f, east, west, up, down, now))


def at(j):
    return slice(128 * j, 128 * j + 128)


def table(shape):
    return pl.BlockSpec(shape, lambda *args: (0,) * len(shape))


def pack_static(ids, scal, vx, vy, target, forcing):
    levels, rows, nx = target.shape

    def body(q, s, u_ref, v_ref, t_ref, w_ref, up_ref, down_ref):
        for ref, r in ((up_ref, rows - 1), (down_ref, 0)):
            for l in range(2):
                ref[l : l + 1] = u_ref[l, r : r + 1]
                ref[2 + l : 3 + l] = v_ref[l, r : r + 1]
            for l in range(levels):
                nt = s[8 + l] * t_ref[l, r : r + 1]
                for m in range(2):
                    w = w_ref[0, m, l, r : r + 1].astype(F32)
                    i = 4 + m * levels + l
                    ref[i : i + 1] = nt + forcing_scale * w

    shape = (4 + 2 * levels, nx)
    pair = pl.BlockSpec((2, rows, nx), lambda i, q, s: (q[8], 0, 0))
    out = jax.ShapeDtypeStruct(shape, F32)
    return pl.pallas_call(
        body,
        name="pack_static",
        out_shape=(out, out),
        grid_spec=pltpu.PrefetchScalarGridSpec(
            num_scalar_prefetch=2,
            grid=(1,),
            in_specs=[pair, pair, table(target.shape), table((1,) + forcing.shape[1:])],
            out_specs=[table(shape)] * 2,
        ),
        compiler_params=params(16),
        cost_estimate=cost(0, 16 * target.size),
    )(ids, scal, vx, vy, target, forcing)


def pack_edges(ids, parts, limit):
    rows, nx = parts[0].shape[2:]
    total = 8 * len(parts)

    def body(s, *refs):
        up_ref, down_ref = refs[-2:]
        for p, f_ref in enumerate(refs[:-2]):
            for m in range(2):
                for l in range(2):
                    i = ((2 * p + m) * 2 + l) * 2
                    up_ref[i : i + 2] = f_ref[m, l, rows - 2 : rows]
                    down_ref[i : i + 2] = f_ref[m, l, 0:2]

    block = (2, 2, rows, nx)
    in_specs = []
    for part in parts:
        if part.shape[1] == 2:
            in_specs.append(table(block))
        else:
            in_specs.append(pl.BlockSpec(block, lambda i, s: (0, s[8], 0, 0)))
    out = jax.ShapeDtypeStruct((total, nx), F32)
    return pl.pallas_call(
        body,
        name="pack_edges",
        out_shape=(out, out),
        grid_spec=pltpu.PrefetchScalarGridSpec(
            num_scalar_prefetch=1,
            grid=(1,),
            in_specs=in_specs,
            out_specs=[table((total, nx))] * 2,
        ),
        compiler_params=params(limit),
        cost_estimate=cost(0, len(parts) * 16 * rows * nx),
    )(ids, *parts)


def twice(ids, scal, parts, vx, vy, halo, static, before):
    _, rows, nx = vx.shape
    lanes = nx // 128
    base = 0 if before is None else 2

    def body(q, s, f0_ref, f1_ref, u_ref, v_ref, below_ref, above_ref, sb_ref, sa_ref, *rest):
        out_ref, cur_ref, mid_ref, low_ref, high_ref = rest[-5:]
        l, p = pl.program_id(0), pl.program_id(1)
        level = 2 * q[8] + l
        d, nu = s[level], s[8 + level]
        low_ok = s[16] > 0.0
        high_ok = s[17] > 0.0

        @pl.when(p == 0)
        def _():
            cur_ref[...] = f0_ref[:, 0]

        @pl.when(p == 1)
        def _():
            cur_ref[...] = f1_ref[:, 0]

        def edge_row(ref, f, n, so):
            u = ref[pl.ds(l, 1), :]
            v = ref[pl.ds(2 + l, 1), :]
            east = pltpu.roll(f, nx - 1, 1)
            west = pltpu.roll(f, 1, 1)
            return combine(f, east, west, n, so, coefs_of(d, nu, u, v))

        for m in range(2):
            here = ((2 * p + m) * 2 + l) * 2
            s2 = below_ref[pl.ds(here, 1), :]
            s1 = below_ref[pl.ds(here + 1, 1), :]
            n1 = above_ref[pl.ds(here, 1), :]
            n2 = above_ref[pl.ds(here + 1, 1), :]
            new_low = edge_row(sb_ref, s1, cur_ref[m, 0:1, :], s2)
            new_high = edge_row(sa_ref, n1, n2, cur_ref[m, rows - 1 : rows, :])
            low_ref[0, m] = jnp.where(low_ok, s1, 0.0)
            high_ref[0, m] = jnp.where(high_ok, n1, 0.0)
            low_ref[1, m] = jnp.where(low_ok, new_low, 0.0)
            high_ref[1, m] = jnp.where(high_ok, new_high, 0.0)

        def coefs(j):
            return coefs_of(d, nu, u_ref[0, :, at(j)], v_ref[0, :, at(j)])

        for step in range(2):

            def load(m, j):
                return mid_ref[m, :, at(j)] if step else cur_ref[m, :, at(j)]

            def edges(m, j):
                return low_ref[step, m, :, at(j)], high_ref[step, m, :, at(j)]

            def emit(m, j, value):
                if step:
                    out_ref[m, 0, :, at(j)] = value
                else:
                    mid_ref[m, :, at(j)] = value

            sweep(load, edges, coefs, emit, 2, lanes, rows)

    one = pl.BlockSpec((1, rows, nx), lambda l, p, q, s: (2 * q[8] + l, 0, 0))
    part_specs = []
    for part in parts:
        if part.shape[1] == 2:
            part_specs.append(pl.BlockSpec((2, 1, rows, nx), lambda l, p, q, s: (0, l, 0, 0)))
        else:
            part_specs.append(
                pl.BlockSpec((2, 1, rows, nx), lambda l, p, q, s: (0, 2 * q[8] + l, 0, 0))
            )
    in_specs = part_specs + [one, one] + [table(h.shape) for h in (*halo, *static)]
    args = [ids, scal, *parts, vx, vy, *halo, *static]
    aliases = {}
    if before is not None:
        aliases = {len(args): 0}
        in_specs.append(pl.BlockSpec(memory_space=pl.ANY))
        args.append(before)
    return pl.pallas_call(
        body,
        name="twice",
        out_shape=jax.ShapeDtypeStruct((8, 2, rows, nx), F32),
        grid_spec=pltpu.PrefetchScalarGridSpec(
            num_scalar_prefetch=2,
            grid=(2, 2),
            in_specs=in_specs,
            out_specs=pl.BlockSpec((2, 1, rows, nx), lambda l, p, q, s: (base + p, l, 0, 0)),
            scratch_shapes=[
                pltpu.VMEM((2, rows, nx), F32),
                pltpu.VMEM((2, rows, nx), F32),
                pltpu.VMEM((2, 2, 1, nx), F32),
                pltpu.VMEM((2, 2, 1, nx), F32),
            ],
        ),
        input_output_aliases=aliases,
        compiler_params=params(16),
        cost_estimate=cost(60 * 8 * rows * nx, 96 * rows * nx),
    )(*args)


def driven(ids, scal, vx, vy, target, forcing, below, above):
    level_count, rows, nx = target.shape
    lanes = nx // 128

    def body(q, s, u_ref, v_ref, t_ref, w_ref, below_ref, above_ref, *rest):
        outs, (src_ref, res_ref, low_ref, high_ref) = rest[:4], rest[4:]
        k, l = 3 - pl.program_id(0), pl.program_id(1)
        level = 2 * (q[8] ^ k) + l
        d, nu = s[level], s[8 + level]
        for m in range(2):
            row = pl.ds(4 + m * level_count + level, 1)
            low_ref[m] = jnp.where(s[16] > 0.0, below_ref[row, :], 0.0)
            high_ref[m] = jnp.where(s[17] > 0.0, above_ref[row, :], 0.0)
        for j in range(lanes):
            nt = nu * t_ref[0, :, at(j)]
            for m in range(2):
                src_ref[m, :, at(j)] = nt + forcing_scale * w_ref[0, m, 0, :, at(j)].astype(F32)

        def coefs(j):
            return coefs_of(d, nu, u_ref[0, :, at(j)], v_ref[0, :, at(j)])

        def load(m, j):
            return src_ref[m, :, at(j)]

        def edges(m, j):
            return low_ref[m, :, at(j)], high_ref[m, :, at(j)]

        def emit(m, j, value):
            later = nu * t_ref[0, :, at(j)] + forcing_scale * w_ref[1, m, 0, :, at(j)].astype(F32)
            res_ref[m, :, at(j)] = value + later

        sweep(load, edges, coefs, emit, 2, lanes, rows)
        for value in range(4):

            @pl.when(k == value)
            def _(ref=outs[value]):
                ref[:, 0] = res_ref[...]

    def turn(value):
        def index(k, l, q, s):
            k = 3 - k
            return (0, jnp.where(k == value, l, jnp.where(k > value, 0, 1)), 0, 0)

        return index

    group = lambda k, l, q: 2 * (q[8] ^ (3 - k)) + l
    one = pl.BlockSpec((1, rows, nx), lambda k, l, q, s: (group(k, l, q), 0, 0))
    return pl.pallas_call(
        body,
        name="driven",
        out_shape=[jax.ShapeDtypeStruct((2, 2, rows, nx), F32)] * 4,
        grid_spec=pltpu.PrefetchScalarGridSpec(
            num_scalar_prefetch=2,
            grid=(4, 2),
            in_specs=[
                one,
                one,
                one,
                pl.BlockSpec(
                    (2, 2, 1, rows, nx), lambda k, l, q, s: (0, 0, group(k, l, q), 0, 0)
                ),
                table(below.shape),
                table(above.shape),
            ],
            out_specs=[pl.BlockSpec((2, 1, rows, nx), turn(value)) for value in range(4)],
            scratch_shapes=[
                pltpu.VMEM((2, rows, nx), F32),
                pltpu.VMEM((2, rows, nx), F32),
                pltpu.VMEM((2, 1, nx), F32),
                pltpu.VMEM((2, 1, nx), F32),
            ],
        ),
        compiler_params=params(16),
        cost_estimate=cost(40 * 2 * target.size, 28 * target.size),
    )(ids, scal, vx, vy, target, forcing, below, above)


def slot(ids, k, m):
    member = ids[2 * (ids[8] ^ k) + m]
    return 2 * ((member >> 1) ^ ids[8]) + (member & 1)


def assemble(ids, moved, rests, tiles, base, before):
    _, _, rows, nx = moved.shape
    cols = nx // tiles
    per = 128 // cols

    def body(s, f0_ref, f1_ref, r0_ref, r1_ref, *rest):
        out_ref, sum_ref = rest[-2:]
        k = pl.program_id(0)
        lane = lax.broadcasted_iota(jnp.int32, (rows, 128), 1)
        for value, ref in enumerate((r0_ref, r1_ref)):

            @pl.when(k == value)
            def _(ref=ref):
                sum_ref[0] = f0_ref[0] + ref[0]
                sum_ref[1] = f1_ref[0] + ref[1]

        for j in range(nx // 128):
            pieces = [sum_ref[m, l, :, at(j)] for m in range(2) for l in range(2)]
            for q in range(per):
                block = None
                for i in range(4):
                    shift = ((i - q) * cols) % 128
                    moved = pltpu.roll(pieces[i], shift, 1) if shift else pieces[i]
                    block = moved if block is None else jnp.where(lane >= i * cols, moved, block)
                out_ref[0, per * j + q] = block

    one = (1, 2, rows, nx)
    in_specs = [
        pl.BlockSpec(one, lambda k, s: (slot(s, base + k, 0), 0, 0, 0)),
        pl.BlockSpec(one, lambda k, s: (slot(s, base + k, 1), 0, 0, 0)),
    ] + [table((2, 2, rows, nx))] * 2
    args = [ids, moved, moved, *rests]
    aliases = {}
    if before is not None:
        aliases = {len(args): 0}
        in_specs.append(pl.BlockSpec(memory_space=pl.ANY))
        args.append(before)
    return pl.pallas_call(
        body,
        name="assemble",
        out_shape=jax.ShapeDtypeStruct((4, tiles, rows, 128), F32),
        grid_spec=pltpu.PrefetchScalarGridSpec(
            num_scalar_prefetch=1,
            grid=(2,),
            in_specs=in_specs,
            out_specs=pl.BlockSpec((1, tiles, rows, 128), lambda k, s: (s[8] ^ (base + k), 0, 0, 0)),
            scratch_shapes=[pltpu.VMEM((2, 2, rows, nx), F32)],
        ),
        input_output_aliases=aliases,
        compiler_params=params(20),
        cost_estimate=cost(moved.size, 8 * moved.size),
    )(*args)


def finish(depths, arrived, ny):
    pairs, tiles, rows, _ = arrived.shape
    levels = 2 * pairs
    group = 128 // rows
    blocks = 2 if tiles % (2 * group) == 0 else 1
    steps = tiles // (group * blocks)
    width = 128 * blocks
    scale = ny ** (-0.5)

    def body(s, a_ref, out_ref, sum_ref, carry):
        @pl.when(pl.program_id(0) == 0)
        def _():
            carry[...] = jnp.zeros_like(carry)

        r = lax.broadcasted_iota(jnp.int32, (128, 128), 0)
        c = lax.broadcasted_iota(jnp.int32, (128, 128), 1)
        tri = (r <= c).astype(jnp.bfloat16)
        for b in range(blocks):
            lanes = slice(128 * b, 128 * b + 128)
            total = None
            for lp in range(pairs):
                x = a_ref[lp, group * b : group * (b + 1)].reshape(128, 128).T
                x = x.reshape(2, 2, 32, 128)
                for k in range(2):
                    level = 2 * lp + k
                    out_ref[:, level, :, lanes] = x[:, k]
                    term = s[level] * x[:, k]
                    total = term if total is None else total + term
            total = total.reshape(64, 128)
            hi = total.astype(jnp.bfloat16)
            lo = (total - hi.astype(F32)).astype(jnp.bfloat16)
            run = jnp.dot(hi, tri, preferred_element_type=F32) + jnp.dot(
                lo, tri, preferred_element_type=F32
            )
            run = run + carry[...]
            carry[...] = jnp.broadcast_to(run[:, 127:128], (64, 128))
            sum_ref[:, :, lanes] = (run * scale).reshape(2, 32, 128)

    return pl.pallas_call(
        body,
        name="finish",
        out_shape=(
            jax.ShapeDtypeStruct((2, levels, 32, ny), F32),
            jax.ShapeDtypeStruct((2, 32, ny), F32),
        ),
        grid_spec=pltpu.PrefetchScalarGridSpec(
            num_scalar_prefetch=1,
            grid=(steps,),
            in_specs=[pl.BlockSpec((pairs, group * blocks, rows, 128), lambda i, s: (0, i, 0, 0))],
            out_specs=[
                pl.BlockSpec((2, levels, 32, width), lambda i, s: (0, 0, 0, i)),
                pl.BlockSpec((2, 32, width), lambda i, s: (0, 0, i)),
            ],
            scratch_shapes=[pltpu.VMEM((64, 128), F32)],
        ),
        compiler_params=params(16),
        cost_estimate=cost(20 * arrived.size, 12 * arrived.size),
    )(depths, arrived)


def on_device(
    ensemble,
    owners,
    velocity_x,
    northward_speed_ratio,
    target,
    forcing,
    diffusion,
    nudging,
    level_depths,
):
    tiles = lax.axis_size("tile")
    rows, _ = ensemble.shape[2:]
    group = lax.axis_index("particle")
    tile = lax.axis_index("tile")
    up = [(i, (i + 1) % tiles) for i in range(tiles)]
    down = [(j, i) for i, j in up]

    def trade(value, k):
        return lax.ppermute(value, "particle", [(i, i ^ k) for i in range(4)])

    pieces = [lax.dynamic_slice_in_dim(ensemble, 2 * (group ^ k), 2, axis=1) for k in range(4)]
    parts = [pieces[0], None, None, None]
    for k in (3, 2, 1):
        parts[k] = trade(pieces[k], k)

    ids = jnp.concatenate([owners, group[None].astype(jnp.int32)])
    edges_ok = jnp.stack([tile > 0, tile < tiles - 1]).astype(F32)
    scal = jnp.concatenate([diffusion, nudging, edges_ok])

    def exchange(pair):
        below = lax.ppermute(pair[0], "tile", up)
        above = lax.ppermute(pair[1], "tile", down)
        return below, above

    edges = pack_static(ids, scal, velocity_x, northward_speed_ratio, target, forcing)
    static = exchange(edges)
    edges = pack_edges(ids, parts[:2], 16)
    near = exchange(edges)
    rests = driven(
        ids, scal, velocity_x, northward_speed_ratio, target, forcing, *static
    )
    rests = list(rests)
    for k in (3, 2, 1):
        rests[k] = trade(rests[k], k)
    edges = pack_edges(ids, parts[2:], 16)
    far = exchange(edges)
    moved = twice(
        ids, scal, parts[:2], velocity_x, northward_speed_ratio, near, static, None
    )
    moved = twice(
        ids, scal, parts[2:], velocity_x, northward_speed_ratio, far, static, moved
    )
    blocks = assemble(ids, moved, rests[:2], tiles, 0, None)
    blocks = assemble(ids, moved, rests[2:], tiles, 2, blocks)
    arrived = lax.all_to_all(
        blocks.reshape(4 * tiles, rows, 128), ("particle", "tile"), 0, 0, tiled=True
    )
    return finish(level_depths, arrived.reshape(4, tiles, rows, 128), tiles * rows)


def solution(mesh):
    placed = (
        P("particle", None, "tile", None),
        P(),
        P(None, "tile", None),
        P(None, "tile", None),
        P(None, "tile", None),
        P(None, "particle", None, "tile", None),
        P(),
        P(),
        P(),
    )
    return jax.shard_map(
        on_device,
        mesh=mesh,
        in_specs=placed,
        out_specs=(P("particle", None, "tile", None), P("particle", "tile", None)),
        check_vma=False,
    )
```

```python
import jax
import jax.numpy as jnp
from jax import lax
from jax.experimental import pallas as pl
from jax.experimental.pallas import tpu as pltpu
from jax.sharding import PartitionSpec as P


forcing_scale = 0.5
F32 = jnp.float32
MIB = 1 << 20


def params(limit):
    return pltpu.CompilerParams(vmem_limit_bytes=limit * MIB)


def cost(flops, nbytes):
    return pl.CostEstimate(flops=flops, bytes_accessed=nbytes, transcendentals=0)


def combine(f, east, west, n, so, coefs):
    cc, ce, cw, cn, cs = coefs
    return cc * f + (ce * east + cw * west) + (cn * n + cs * so)


def coefs_of(d, nu, u, v):
    hu = 0.5 * u
    hv = 0.5 * v
    return 1.0 - 4.0 * d - nu, d - hu, d + hu, d - hv, d + hv


def sweep(load, edges, coefs, emit, count, lanes, rows):
    row_id = lax.broadcasted_iota(jnp.int32, (rows, 128), 0)
    lane = lax.broadcasted_iota(jnp.int32, (rows, 128), 1)
    turned = []
    for m in range(count):
        last, first = load(m, lanes - 1), load(m, 0)
        turned.append((first, pltpu.roll(last, 1, 1), pltpu.roll(first, 127, 1), pltpu.roll(first, 1, 1)))
    for j in range(lanes):
        now = coefs(j)
        for m in range(count):
            f, prev_right, here_left, here_right = turned[m]
            following = load(m, (j + 1) % lanes)
            next_left = pltpu.roll(following, 127, 1)
            next_right = pltpu.roll(following, 1, 1)
            east = jnp.where(lane == 127, next_left, here_left)
            west = jnp.where(lane == 0, prev_right, here_right)
            turned[m] = (following, here_right, next_left, next_right)
            low, high = edges(m, j)
            up = jnp.where(row_id == rows - 1, high, pltpu.roll(f, rows - 1, 0))
            down = jnp.where(row_id == 0, low, pltpu.roll(f, 1, 0))
            emit(m, j, combine(f, east, west, up, down, now))


def at(j):
    return slice(128 * j, 128 * j + 128)


def table(shape):
    return pl.BlockSpec(shape, lambda *args: (0,) * len(shape))


def pack_static(ids, scal, vx, vy, target, forcing):
    levels, rows, nx = target.shape

    def body(q, s, u_ref, v_ref, t_ref, w_ref, up_ref, down_ref):
        for ref, r in ((up_ref, rows - 1), (down_ref, 0)):
            for l in range(2):
                ref[l : l + 1] = u_ref[l, r : r + 1]
                ref[2 + l : 3 + l] = v_ref[l, r : r + 1]
            for l in range(levels):
                nt = s[8 + l] * t_ref[l, r : r + 1]
                for m in range(2):
                    w = w_ref[0, m, l, r : r + 1].astype(F32)
                    i = 4 + m * levels + l
                    ref[i : i + 1] = nt + forcing_scale * w

    shape = (4 + 2 * levels, nx)
    pair = pl.BlockSpec((2, rows, nx), lambda i, q, s: (q[8], 0, 0))
    out = jax.ShapeDtypeStruct(shape, F32)
    return pl.pallas_call(
        body,
        name="pack_static",
        out_shape=(out, out),
        grid_spec=pltpu.PrefetchScalarGridSpec(
            num_scalar_prefetch=2,
            grid=(1,),
            in_specs=[pair, pair, table(target.shape), table((1,) + forcing.shape[1:])],
            out_specs=[table(shape)] * 2,
        ),
        compiler_params=params(16),
        cost_estimate=cost(0, 16 * target.size),
    )(ids, scal, vx, vy, target, forcing)


def pack_edges(ids, parts, limit):
    rows, nx = parts[0].shape[2:]
    total = 8 * len(parts)

    def body(s, *refs):
        up_ref, down_ref = refs[-2:]
        for p, f_ref in enumerate(refs[:-2]):
            for m in range(2):
                for l in range(2):
                    i = ((2 * p + m) * 2 + l) * 2
                    up_ref[i : i + 2] = f_ref[m, l, rows - 2 : rows]
                    down_ref[i : i + 2] = f_ref[m, l, 0:2]

    block = (2, 2, rows, nx)
    in_specs = []
    for part in parts:
        if part.shape[1] == 2:
            in_specs.append(table(block))
        else:
            in_specs.append(pl.BlockSpec(block, lambda i, s: (0, s[8], 0, 0)))
    out = jax.ShapeDtypeStruct((total, nx), F32)
    return pl.pallas_call(
        body,
        name="pack_edges",
        out_shape=(out, out),
        grid_spec=pltpu.PrefetchScalarGridSpec(
            num_scalar_prefetch=1,
            grid=(1,),
            in_specs=in_specs,
            out_specs=[table((total, nx))] * 2,
        ),
        compiler_params=params(limit),
        cost_estimate=cost(0, len(parts) * 16 * rows * nx),
    )(ids, *parts)


def twice(ids, scal, parts, vx, vy, halo, static, before):
    _, rows, nx = vx.shape
    lanes = nx // 128
    base = 0 if before is None else 2

    def body(q, s, f0_ref, f1_ref, u_ref, v_ref, below_ref, above_ref, sb_ref, sa_ref, *rest):
        out_ref, cur_ref, mid_ref, low_ref, high_ref = rest[-5:]
        l, p = pl.program_id(0), pl.program_id(1)
        level = 2 * q[8] + l
        d, nu = s[level], s[8 + level]
        low_ok = s[16] > 0.0
        high_ok = s[17] > 0.0

        @pl.when(p == 0)
        def _():
            cur_ref[...] = f0_ref[:, 0]

        @pl.when(p == 1)
        def _():
            cur_ref[...] = f1_ref[:, 0]

        def edge_row(ref, f, n, so):
            u = ref[pl.ds(l, 1), :]
            v = ref[pl.ds(2 + l, 1), :]
            east = pltpu.roll(f, nx - 1, 1)
            west = pltpu.roll(f, 1, 1)
            return combine(f, east, west, n, so, coefs_of(d, nu, u, v))

        for m in range(2):
            here = ((2 * p + m) * 2 + l) * 2
            s2 = below_ref[pl.ds(here, 1), :]
            s1 = below_ref[pl.ds(here + 1, 1), :]
            n1 = above_ref[pl.ds(here, 1), :]
            n2 = above_ref[pl.ds(here + 1, 1), :]
            new_low = edge_row(sb_ref, s1, cur_ref[m, 0:1, :], s2)
            new_high = edge_row(sa_ref, n1, n2, cur_ref[m, rows - 1 : rows, :])
            low_ref[0, m] = jnp.where(low_ok, s1, 0.0)
            high_ref[0, m] = jnp.where(high_ok, n1, 0.0)
            low_ref[1, m] = jnp.where(low_ok, new_low, 0.0)
            high_ref[1, m] = jnp.where(high_ok, new_high, 0.0)

        def coefs(j):
            return coefs_of(d, nu, u_ref[0, :, at(j)], v_ref[0, :, at(j)])

        for step in range(2):

            def load(m, j):
                return mid_ref[m, :, at(j)] if step else cur_ref[m, :, at(j)]

            def edges(m, j):
                return low_ref[step, m, :, at(j)], high_ref[step, m, :, at(j)]

            def emit(m, j, value):
                if step:
                    out_ref[m, 0, :, at(j)] = value
                else:
                    mid_ref[m, :, at(j)] = value

            sweep(load, edges, coefs, emit, 2, lanes, rows)

    one = pl.BlockSpec((1, rows, nx), lambda l, p, q, s: (2 * q[8] + l, 0, 0))
    part_specs = []
    for part in parts:
        if part.shape[1] == 2:
            part_specs.append(pl.BlockSpec((2, 1, rows, nx), lambda l, p, q, s: (0, l, 0, 0)))
        else:
            part_specs.append(
                pl.BlockSpec((2, 1, rows, nx), lambda l, p, q, s: (0, 2 * q[8] + l, 0, 0))
            )
    in_specs = part_specs + [one, one] + [table(h.shape) for h in (*halo, *static)]
    args = [ids, scal, *parts, vx, vy, *halo, *static]
    aliases = {}
    if before is not None:
        aliases = {len(args): 0}
        in_specs.append(pl.BlockSpec(memory_space=pl.ANY))
        args.append(before)
    return pl.pallas_call(
        body,
        name="twice",
        out_shape=jax.ShapeDtypeStruct((8, 2, rows, nx), F32),
        grid_spec=pltpu.PrefetchScalarGridSpec(
            num_scalar_prefetch=2,
            grid=(2, 2),
            in_specs=in_specs,
            out_specs=pl.BlockSpec((2, 1, rows, nx), lambda l, p, q, s: (base + p, l, 0, 0)),
            scratch_shapes=[
                pltpu.VMEM((2, rows, nx), F32),
                pltpu.VMEM((2, rows, nx), F32),
                pltpu.VMEM((2, 2, 1, nx), F32),
                pltpu.VMEM((2, 2, 1, nx), F32),
            ],
        ),
        input_output_aliases=aliases,
        compiler_params=params(16),
        cost_estimate=cost(60 * 8 * rows * nx, 96 * rows * nx),
    )(*args)


def driven(ids, scal, vx, vy, target, forcing, below, above):
    level_count, rows, nx = target.shape
    lanes = nx // 128

    def body(q, s, u_ref, v_ref, t_ref, w_ref, below_ref, above_ref, *rest):
        outs, (src_ref, res_ref, low_ref, high_ref) = rest[:4], rest[4:]
        k, l = 3 - pl.program_id(0), pl.program_id(1)
        level = 2 * (q[8] ^ k) + l
        d, nu = s[level], s[8 + level]
        for m in range(2):
            row = pl.ds(4 + m * level_count + level, 1)
            low_ref[m] = jnp.where(s[16] > 0.0, below_ref[row, :], 0.0)
            high_ref[m] = jnp.where(s[17] > 0.0, above_ref[row, :], 0.0)
        for j in range(lanes):
            nt = nu * t_ref[0, :, at(j)]
            for m in range(2):
                src_ref[m, :, at(j)] = nt + forcing_scale * w_ref[0, m, 0, :, at(j)].astype(F32)

        def coefs(j):
            return coefs_of(d, nu, u_ref[0, :, at(j)], v_ref[0, :, at(j)])

        def load(m, j):
            return src_ref[m, :, at(j)]

        def edges(m, j):
            return low_ref[m, :, at(j)], high_ref[m, :, at(j)]

        def emit(m, j, value):
            later = nu * t_ref[0, :, at(j)] + forcing_scale * w_ref[1, m, 0, :, at(j)].astype(F32)
            res_ref[m, :, at(j)] = value + later

        sweep(load, edges, coefs, emit, 2, lanes, rows)
        for value in range(4):

            @pl.when(k == value)
            def _(ref=outs[value]):
                ref[:, 0] = res_ref[...]

    def turn(value):
        def index(k, l, q, s):
            k = 3 - k
            return (0, jnp.where(k == value, l, jnp.where(k > value, 0, 1)), 0, 0)

        return index

    group = lambda k, l, q: 2 * (q[8] ^ (3 - k)) + l
    one = pl.BlockSpec((1, rows, nx), lambda k, l, q, s: (group(k, l, q), 0, 0))
    return pl.pallas_call(
        body,
        name="driven",
        out_shape=[jax.ShapeDtypeStruct((2, 2, rows, nx), F32)] * 4,
        grid_spec=pltpu.PrefetchScalarGridSpec(
            num_scalar_prefetch=2,
            grid=(4, 2),
            in_specs=[
                one,
                one,
                one,
                pl.BlockSpec(
                    (2, 2, 1, rows, nx), lambda k, l, q, s: (0, 0, group(k, l, q), 0, 0)
                ),
                table(below.shape),
                table(above.shape),
            ],
            out_specs=[pl.BlockSpec((2, 1, rows, nx), turn(value)) for value in range(4)],
            scratch_shapes=[
                pltpu.VMEM((2, rows, nx), F32),
                pltpu.VMEM((2, rows, nx), F32),
                pltpu.VMEM((2, 1, nx), F32),
                pltpu.VMEM((2, 1, nx), F32),
            ],
        ),
        compiler_params=params(16),
        cost_estimate=cost(40 * 2 * target.size, 28 * target.size),
    )(ids, scal, vx, vy, target, forcing, below, above)


def slot(ids, k, m):
    member = ids[2 * (ids[8] ^ k) + m]
    return 2 * ((member >> 1) ^ ids[8]) + (member & 1)


def assemble(ids, moved, rests, tiles, base, before):
    _, _, rows, nx = moved.shape
    cols = nx // tiles
    per = 128 // cols

    def body(s, f0_ref, f1_ref, r0_ref, r1_ref, *rest):
        out_ref, sum_ref = rest[-2:]
        k = pl.program_id(0)
        lane = lax.broadcasted_iota(jnp.int32, (rows, 128), 1)
        for value, ref in enumerate((r0_ref, r1_ref)):

            @pl.when(k == value)
            def _(ref=ref):
                sum_ref[0] = f0_ref[0] + ref[0]
                sum_ref[1] = f1_ref[0] + ref[1]

        for j in range(nx // 128):
            pieces = [sum_ref[m, l, :, at(j)] for m in range(2) for l in range(2)]
            for q in range(per):
                block = None
                for i in range(4):
                    shift = ((i - q) * cols) % 128
                    moved = pltpu.roll(pieces[i], shift, 1) if shift else pieces[i]
                    block = moved if block is None else jnp.where(lane >= i * cols, moved, block)
                out_ref[0, per * j + q] = block

    one = (1, 2, rows, nx)
    in_specs = [
        pl.BlockSpec(one, lambda k, s: (slot(s, base + k, 0), 0, 0, 0)),
        pl.BlockSpec(one, lambda k, s: (slot(s, base + k, 1), 0, 0, 0)),
    ] + [table((2, 2, rows, nx))] * 2
    args = [ids, moved, moved, *rests]
    aliases = {}
    if before is not None:
        aliases = {len(args): 0}
        in_specs.append(pl.BlockSpec(memory_space=pl.ANY))
        args.append(before)
    return pl.pallas_call(
        body,
        name="assemble",
        out_shape=jax.ShapeDtypeStruct((4, tiles, rows, 128), F32),
        grid_spec=pltpu.PrefetchScalarGridSpec(
            num_scalar_prefetch=1,
            grid=(2,),
            in_specs=in_specs,
            out_specs=pl.BlockSpec((1, tiles, rows, 128), lambda k, s: (s[8] ^ (base + k), 0, 0, 0)),
            scratch_shapes=[pltpu.VMEM((2, 2, rows, nx), F32)],
        ),
        input_output_aliases=aliases,
        compiler_params=params(20),
        cost_estimate=cost(moved.size, 8 * moved.size),
    )(*args)


def finish(depths, arrived, ny):
    pairs, tiles, rows, _ = arrived.shape
    levels = 2 * pairs
    group = 128 // rows
    blocks = 2 if tiles % (2 * group) == 0 else 1
    steps = tiles // (group * blocks)
    width = 128 * blocks
    scale = ny ** (-0.5)

    def body(s, a_ref, out_ref, sum_ref, carry):
        @pl.when(pl.program_id(0) == 0)
        def _():
            carry[...] = jnp.zeros_like(carry)

        r = lax.broadcasted_iota(jnp.int32, (128, 128), 0)
        c = lax.broadcasted_iota(jnp.int32, (128, 128), 1)
        tri = (r <= c).astype(jnp.bfloat16)
        for b in range(blocks):
            lanes = slice(128 * b, 128 * b + 128)
            total = None
            for lp in range(pairs):
                x = a_ref[lp, group * b : group * (b + 1)].reshape(128, 128).T
                x = x.reshape(2, 2, 32, 128)
                for k in range(2):
                    level = 2 * lp + k
                    out_ref[:, level, :, lanes] = x[:, k]
                    term = s[level] * x[:, k]
                    total = term if total is None else total + term
            total = total.reshape(64, 128)
            hi = total.astype(jnp.bfloat16)
            lo = (total - hi.astype(F32)).astype(jnp.bfloat16)
            run = jnp.dot(hi, tri, preferred_element_type=F32) + jnp.dot(
                lo, tri, preferred_element_type=F32
            )
            run = run + carry[...]
            carry[...] = jnp.broadcast_to(run[:, 127:128], (64, 128))
            sum_ref[:, :, lanes] = (run * scale).reshape(2, 32, 128)

    return pl.pallas_call(
        body,
        name="finish",
        out_shape=(
            jax.ShapeDtypeStruct((2, levels, 32, ny), F32),
            jax.ShapeDtypeStruct((2, 32, ny), F32),
        ),
        grid_spec=pltpu.PrefetchScalarGridSpec(
            num_scalar_prefetch=1,
            grid=(steps,),
            in_specs=[pl.BlockSpec((pairs, group * blocks, rows, 128), lambda i, s: (0, i, 0, 0))],
            out_specs=[
                pl.BlockSpec((2, levels, 32, width), lambda i, s: (0, 0, 0, i)),
                pl.BlockSpec((2, 32, width), lambda i, s: (0, 0, i)),
            ],
            scratch_shapes=[pltpu.VMEM((64, 128), F32)],
        ),
        compiler_params=params(16),
        cost_estimate=cost(20 * arrived.size, 12 * arrived.size),
    )(depths, arrived)


def on_device(
    ensemble,
    owners,
    velocity_x,
    northward_speed_ratio,
    target,
    forcing,
    diffusion,
    nudging,
    level_depths,
):
    tiles = lax.axis_size("tile")
    rows, _ = ensemble.shape[2:]
    group = lax.axis_index("particle")
    tile = lax.axis_index("tile")
    up = [(i, (i + 1) % tiles) for i in range(tiles)]
    down = [(j, i) for i, j in up]

    def trade(value, k):
        return lax.ppermute(value, "particle", [(i, i ^ k) for i in range(4)])

    def cut(value, k):
        return lax.dynamic_slice_in_dim(value, 2 * (group ^ k), 2, axis=1)

    parts = [None] * 4
    pieces = (cut(ensemble, 2), cut(ensemble, 3))
    held, *pieces = lax.optimization_barrier((ensemble, *pieces))
    pieces = [cut(held, 0), cut(held, 1), *pieces]
    parts[0] = pieces[0]
    for k in (3, 2, 1):
        parts[k] = trade(pieces[k], k)

    ids = jnp.concatenate([owners, group[None].astype(jnp.int32)])
    edges_ok = jnp.stack([tile > 0, tile < tiles - 1]).astype(F32)
    scal = jnp.concatenate([diffusion, nudging, edges_ok])

    def exchange(pair):
        below = lax.ppermute(pair[0], "tile", up)
        above = lax.ppermute(pair[1], "tile", down)
        return below, above

    edges = pack_static(ids, scal, velocity_x, northward_speed_ratio, target, forcing)
    static = exchange(edges)
    edges = pack_edges(ids, parts[:2], 16)
    near = exchange(edges)
    rests = driven(
        ids, scal, velocity_x, northward_speed_ratio, target, forcing, *static
    )
    rests = list(rests)
    for k in (3, 2, 1):
        rests[k] = trade(rests[k], k)
    edges = pack_edges(ids, parts[2:], 16)
    far = exchange(edges)
    moved = twice(
        ids, scal, parts[:2], velocity_x, northward_speed_ratio, near, static, None
    )
    moved = twice(
        ids, scal, parts[2:], velocity_x, northward_speed_ratio, far, static, moved
    )
    blocks = assemble(ids, moved, rests[:2], tiles, 0, None)
    blocks = assemble(ids, moved, rests[2:], tiles, 2, blocks)
    arrived = lax.all_to_all(
        blocks.reshape(4 * tiles, rows, 128), ("particle", "tile"), 0, 0, tiled=True
    )
    return finish(level_depths, arrived.reshape(4, tiles, rows, 128), tiles * rows)


def solution(mesh):
    placed = (
        P("particle", None, "tile", None),
        P(),
        P(None, "tile", None),
        P(None, "tile", None),
        P(None, "tile", None),
        P(None, "particle", None, "tile", None),
        P(),
        P(),
        P(),
    )
    return jax.shard_map(
        on_device,
        mesh=mesh,
        in_specs=placed,
        out_specs=(P("particle", None, "tile", None), P("particle", "tile", None)),
        check_vma=False,
    )
```
